32 devices in a mesh: rep: 4 (over y, core), tp: 8 (over z, x).
Axes of the slice: x: 2, y: 2, z: 4, core: 2. Of those that a mesh axis runs over, the one named last changes fastest.
Arguments:
- tokens: bfloat16 [4, 192, 6144], P('rep', 'tp'), may hold values from -6 to 6
- cotangent: bfloat16 [4, 192, 6144], P('rep', 'tp'), may hold values from -6 to 6
- w_in: bfloat16 [4, 6144, 12288], P('rep', None, 'tp'), may hold values from -6 to 6
- w_out: bfloat16 [4, 12288, 6144], P('rep', 'tp'), may hold values from -6 to 6
- gossip_step: int32 [1], replicated, may hold values from 0 to 7
Outputs:
- input_grad: bfloat16 [4, 192, 6144], P('rep', 'tp')
- mixed_in: bfloat16 [4, 6144, 12288], P('rep', None, 'tp')
- mixed_out: bfloat16 [4, 12288, 6144], P('rep', 'tp')
The draws below stay inside these ranges and needn't reach their ends.
All inputs are finite; a program needn't handle non-finite values.
Results may differ from the reference program's by a relative error of at most 0.023.
Values may be sent and summed in bfloat16 or wider, within the bound.
No kernel may reach another device: no remote copies, remote signals or barrier semaphores. Data moves between devices by JAX's collectives and lax.ppermute only.
A program may use at most 256 MiB of HBM per device.

```python
import jax
import jax.numpy as jnp
from jax import lax

D = 6144
HID = 12288
TOKENS = 192
N_REP = 4
N_TP = 8


def block_levels(stream_key, dims, cuts, smallest, high):
    level = 1.0
    for position, blocks in cuts:
        draws = jax.random.uniform(jax.random.fold_in(jax.random.fold_in(stream_key, 6), position), (blocks,), jnp.float32, smallest / len(cuts), high / len(cuts))
        level = level * jnp.repeat(jnp.exp(draws), dims[position] // blocks).reshape((-1,) + (1,) * (len(dims) - 1 - position))
    return level


def normal_values(rng, extent, spread, most, shards=(), held_as=jnp.bfloat16):
    values = jax.random.normal(rng, extent, jnp.float32) * spread
    if len(shards) > 0:
        values = block_levels(rng, extent, shards, -0.22, 0.18) * values
    return jnp.clip(values, min=-most, max=most).astype(held_as)


def setup_inputs(seed: int = 0) -> dict:
    splits = jax.random.split(jax.random.key(seed), 6)
    tokens = normal_values(splits[0], (N_REP, TOKENS, D), 1.0, 6.0, ((0, 4), (1, 8)))
    cotangent = normal_values(splits[1], (N_REP, TOKENS, D), 1.0, 6.0, ((0, 4), (1, 8)))
    w_in = normal_values(splits[2], (N_REP, D, HID), 1.0, 6.0, ((0, 4), (2, 8)))
    w_out = normal_values(splits[3], (N_REP, HID, D), 1.0, 6.0, ((0, 4), (1, 8)))
    gossip_step = jax.random.randint(splits[4], (1,), 0, 8).astype(jnp.int32)
    return {"tokens": tokens, "cotangent": cotangent, "w_in": w_in, "w_out": w_out, "gossip_step": gossip_step}


def gelu_parts(preact):
    cdf = 0.5 * (1.0 + lax.erf(preact * 0.7071067811865476))
    dens = jnp.exp(-0.5 * preact * preact) * 0.3989422804014327
    return preact * cdf, cdf + preact * dens


def one_group(tokens, cotangent, w_in, w_out, rate):
    scale_in = 1.0 / (D ** 0.5)
    scale_out = 1.0 / (HID ** 0.5)
    preact = jnp.dot(tokens, w_in, preferred_element_type=jnp.float32) * scale_in
    value, slope = gelu_parts(preact)
    hidden = value.astype(jnp.bfloat16)
    back = jnp.dot(cotangent, w_out.T, preferred_element_type=jnp.float32) * scale_out
    dpre = (back * slope).astype(jnp.bfloat16)
    grad_out = jnp.dot(hidden.T, cotangent, preferred_element_type=jnp.float32) * scale_out
    grad_in = jnp.dot(tokens.T, dpre, preferred_element_type=jnp.float32) * scale_in
    hid_dev = HID // N_TP
    dblocks = dpre.astype(jnp.float32).reshape(TOKENS, N_TP, hid_dev)
    wblocks = w_in.astype(jnp.float32).reshape(D, N_TP, hid_dev)
    partials = (jnp.einsum("tnh,dnh->ntd", dblocks, wblocks) * scale_in).astype(jnp.bfloat16)
    input_grad = jnp.sum(partials.astype(jnp.float32), axis=0).astype(jnp.bfloat16)
    new_in = (w_in.astype(jnp.float32) - rate * grad_in).astype(jnp.bfloat16)
    new_out = (w_out.astype(jnp.float32) - rate * grad_out).astype(jnp.bfloat16)
    return input_grad, new_in, new_out


def reference(tokens, cotangent, w_in, w_out, gossip_step):
    rate = 16.0 / (8.0 + gossip_step[0].astype(jnp.float32))
    grads, ins, outs = [], [], []
    for group in range(N_REP):
        result = one_group(tokens[group], cotangent[group], w_in[group], w_out[group], rate)
        grads.append(result[0])
        ins.append(result[1])
        outs.append(result[2])
    nbits = N_REP.bit_length() - 1
    which = (gossip_step[0] % nbits).astype(jnp.int32)
    distance = jnp.left_shift(jnp.int32(1), which)
    mixed_in, mixed_out = [], []
    stack_in = jnp.stack(ins)
    stack_out = jnp.stack(outs)
    for group in range(N_REP):
        partner = jnp.bitwise_xor(jnp.int32(group), distance)
        other_in = lax.dynamic_index_in_dim(stack_in, partner, 0, keepdims=False)
        other_out = lax.dynamic_index_in_dim(stack_out, partner, 0, keepdims=False)
        mixed_in.append(((ins[group].astype(jnp.float32) + other_in.astype(jnp.float32)) * 0.5).astype(jnp.bfloat16))
        mixed_out.append(((outs[group].astype(jnp.float32) + other_out.astype(jnp.float32)) * 0.5).astype(jnp.bfloat16))
    return jnp.stack(grads), jnp.stack(mixed_in), jnp.stack(mixed_out)
```

```python
from functools import partial

import jax
import jax.numpy as jnp
from jax import lax
from jax.sharding import PartitionSpec as P


def from_partner(value, stride):
    mask = 2**stride
    pairs = [(source, source ^ mask) for source in range(lax.axis_size("rep"))]
    return lax.ppermute(value, "rep", pairs)


def after(value, *earlier):
    return lax.optimization_barrier((value, *earlier))[0]


def gelu_parts(preact):
    cdf = 0.5 * (1.0 + lax.erf(preact * 0.7071067811865476))
    dens = jnp.exp(-0.5 * preact * preact) * 0.3989422804014327
    return (preact * cdf, cdf + preact * dens)


def flip_size():
    return 2 if lax.axis_size("tp") % 2 == 0 else 1


def step_up(value):
    size, inner = lax.axis_size("tp"), flip_size()
    return lax.ppermute(value, "tp", [(i, (i + inner) % size) for i in range(size)])


def flip(value):
    return lax.ppermute(value, "tp", [(i, i ^ 1) for i in range(lax.axis_size("tp"))])


def short_ring():
    return lax.axis_size("tp") // flip_size() <= 4


def gather_slots(shard):
    inner = flip_size()
    ring = lax.axis_size("tp") // inner
    straight, flipped, current = [], [], shard
    for step in range(ring):
        if step:
            current = step_up(current)
        straight.append(current)
        if inner == 2:
            flipped.append(flip(current))
    return straight + flipped


def gather_rows(*shards):
    if not short_ring():
        return [lax.all_gather(shard, "tp", axis=0, tiled=True) for shard in shards]
    rows = shards[0].shape[0]
    slots = gather_slots(jnp.concatenate(shards, axis=0) if len(shards) > 1 else shards[0])
    return [
        jnp.concatenate([slot[n * rows : (n + 1) * rows] for slot in slots], axis=0)
        for n in range(len(shards))
    ]


def scatter_sum(partial_sums, rows):
    if not short_ring():
        return lax.psum_scatter(partial_sums, "tp", scatter_dimension=0, tiled=True)
    inner = flip_size()
    ring = lax.axis_size("tp") // inner
    slot = lambda number: partial_sums[number * rows : (number + 1) * rows]
    arrived = [None] * ring
    if inner == 2:
        arrived = [flip(slot(ring + (k + 1) % ring)) for k in range(ring)]
    carried = None
    for k in range(ring):
        total = slot((k + 1) % ring).astype(jnp.float32)
        if arrived[k] is not None:
            total = total + arrived[k].astype(jnp.float32)
        if carried is not None:
            total = total + carried.astype(jnp.float32)
        carried = total.astype(jnp.bfloat16)
        if k < ring - 1:
            carried = step_up(carried)
    return carried


def dot_tn(left, right):
    return lax.dot_general(
        left, right, (((0,), (0,)), ((), ())), preferred_element_type=jnp.float32
    )


def dot_nt(left, right):
    return lax.dot_general(
        left, right, (((1,), (1,)), ((), ())), preferred_element_type=jnp.float32
    )


def mean_of(own, other):
    return ((own.astype(jnp.float32) + other.astype(jnp.float32)) * 0.5).astype(jnp.bfloat16)


def activations(tokens, upstream, w_in, w_out, scale_in, scale_out):
    preact = jnp.dot(tokens, w_in, preferred_element_type=jnp.float32) * scale_in
    value, slope = gelu_parts(preact)
    back = dot_nt(upstream, w_out) * scale_out
    return value.astype(jnp.bfloat16), (back * slope).astype(jnp.bfloat16)


def near(tok, cot, w_in, w_out, rate, scale_in, scale_out, bit):
    rows = tok.shape[0]
    other_in = from_partner(w_in, bit)
    other_out = from_partner(w_out, bit)
    tokens, upstream = gather_rows(tok, cot)
    hidden, dpre = activations(tokens, upstream, w_in, w_out, scale_in, scale_out)
    partials = (dot_nt(dpre, w_in) * scale_in).astype(jnp.bfloat16)
    input_grad = scatter_sum(partials, rows)
    tokens2 = jnp.concatenate([tokens, from_partner(tokens, bit)], axis=0)
    upstream2 = jnp.concatenate([upstream, from_partner(upstream, bit)], axis=0)
    hidden2 = jnp.concatenate([hidden, from_partner(hidden, bit)], axis=0)
    dpre2 = jnp.concatenate([dpre, from_partner(dpre, bit)], axis=0)

    def finish(own, other, left, right, factor):
        both = own.astype(jnp.float32) + other.astype(jnp.float32)
        return (0.5 * both - factor * dot_tn(left, right)).astype(jnp.bfloat16)

    mixed_in = finish(w_in, other_in, tokens2, dpre2, 0.5 * rate * scale_in)
    mixed_out = finish(w_out, other_out, hidden2, upstream2, 0.5 * rate * scale_out)
    return input_grad, mixed_in, mixed_out


def far(tok, cot, w_in, w_out, rate, scale_in, scale_out, bit):
    rows = tok.shape[0]
    hid = w_in.shape[1]
    unit = hid // 12
    sent = []

    def send(value):
        if len(sent) >= 2:
            value = after(value, sent[-2])
        sent.append(from_partner(value, bit))
        return sent[-1]

    raw_cuts = [(0, unit), (unit, 4 * unit)]
    raw_other = [send(w_in[:, lo:hi]) for lo, hi in raw_cuts[:1]]
    tok_other = from_partner(tok, bit)
    raw_other += [send(w_in[:, lo:hi]) for lo, hi in raw_cuts[1:]]
    raw_hi = raw_cuts[-1][1]

    tokens, upstream = gather_rows(tok, cot)
    hidden, dpre = activations(tokens, upstream, w_in, w_out, scale_in, scale_out)

    def new_in(lo, hi):
        grad = dot_tn(tokens, dpre[:, lo:hi])
        return (w_in[:, lo:hi].astype(jnp.float32) - rate * scale_in * grad).astype(jnp.bfloat16)

    def new_out(lo, hi):
        grad = dot_tn(hidden[:, lo:hi], upstream)
        return (w_out[lo:hi].astype(jnp.float32) - rate * scale_out * grad).astype(jnp.bfloat16)

    mixed_in = jnp.zeros_like(w_in)
    mixed_out = jnp.zeros_like(w_out)
    plan = [
        ("out", 0, 3),
        ("out", 3, 6),
        ("in", 4, 8),
        ("in", 8, 12),
        ("out", 6, 9),
        ("out", 9, 11),
        ("out", 11, 12),
    ]
    dpre_other = None
    tokens_other = None
    for number, (which, lo, hi) in enumerate(plan):
        lo, hi = lo * unit, (hi * unit if hi < 12 else hid)
        own = new_in(lo, hi) if which == "in" else new_out(lo, hi)
        other = send(own)
        if number == 0:
            dpre_other = from_partner(dpre[:, :raw_hi], bit)
        mixed = mean_of(own, other)
        if which == "in":
            mixed_in = lax.dynamic_update_slice(mixed_in, mixed, (0, lo))
        else:
            mixed_out = lax.dynamic_update_slice(mixed_out, mixed, (lo, 0))
        if number == 1:
            held = after(tok_other, mixed)
            tokens_other = gather_rows(held)[0]
            partials = (dot_nt(after(dpre, mixed), w_in) * scale_in).astype(jnp.bfloat16)
            input_grad = scatter_sum(partials, rows)
            tokens2 = jnp.concatenate([tokens, tokens_other], axis=0)
            for (a, b), other_raw in zip(raw_cuts, raw_other):
                dpre2 = jnp.concatenate([dpre[:, a:b], dpre_other[:, a:b]], axis=0)
                both = w_in[:, a:b].astype(jnp.float32) + other_raw.astype(jnp.float32)
                done = 0.5 * both - 0.5 * rate * scale_in * dot_tn(tokens2, dpre2)
                mixed_in = lax.dynamic_update_slice(mixed_in, done.astype(jnp.bfloat16), (0, a))
    return input_grad, mixed_in, mixed_out


def per_device(tokens, cotangent, w_in, w_out, gossip_step):
    width = tokens.shape[2]
    hid_dev = w_in.shape[2]
    scale_in = 1.0 / width**0.5
    scale_out = 1.0 / (hid_dev * lax.axis_size("tp")) ** 0.5
    rate = 16.0 / (8.0 + gossip_step[0].astype(jnp.float32))
    nbits = lax.axis_size("rep").bit_length() - 1
    branches = [
        partial(near if bit == 0 else far, scale_in=scale_in, scale_out=scale_out, bit=bit)
        for bit in range(nbits)
    ]
    input_grad, mixed_in, mixed_out = lax.switch(
        gossip_step[0] % nbits, branches, tokens[0], cotangent[0], w_in[0], w_out[0], rate
    )
    return (input_grad[None], mixed_in[None], mixed_out[None])


def solution(mesh):
    return jax.shard_map(
        per_device,
        mesh=mesh,
        in_specs=(
            P("rep", "tp", None),
            P("rep", "tp", None),
            P("rep", None, "tp"),
            P("rep", "tp", None),
            P(),
        ),
        out_specs=(P("rep", "tp", None), P("rep", None, "tp"), P("rep", "tp", None)),
        check_vma=False,
    )
```

```python
from functools import partial

import jax
import jax.numpy as jnp
from jax import lax
from jax.experimental import pallas as pl
from jax.experimental.pallas import tpu as pltpu
from jax.sharding import PartitionSpec as P


def from_partner(value, stride):
    mask = 2**stride
    pairs = [(source, source ^ mask) for source in range(lax.axis_size("rep"))]
    return lax.ppermute(value, "rep", pairs)


def after(value, *earlier):
    return lax.optimization_barrier((value, *earlier))[0]


def gelu_parts(preact):
    cdf = 0.5 * (1.0 + lax.erf(preact * 0.7071067811865476))
    dens = jnp.exp(-0.5 * preact * preact) * 0.3989422804014327
    return (preact * cdf, cdf + preact * dens)


def flip_size():
    return 2 if lax.axis_size("tp") % 2 == 0 else 1


def step_up(value):
    size, inner = lax.axis_size("tp"), flip_size()
    return lax.ppermute(value, "tp", [(i, (i + inner) % size) for i in range(size)])


def flip(value):
    return lax.ppermute(value, "tp", [(i, i ^ 1) for i in range(lax.axis_size("tp"))])


def short_ring():
    return lax.axis_size("tp") // flip_size() <= 4


def gather_slots(shard):
    inner = flip_size()
    ring = lax.axis_size("tp") // inner
    straight, flipped, current = [], [], shard
    for step in range(ring):
        if step:
            current = step_up(current)
        straight.append(current)
        if inner == 2:
            flipped.append(flip(current))
    return straight + flipped


def gather_rows(*shards):
    if not short_ring():
        return [lax.all_gather(shard, "tp", axis=0, tiled=True) for shard in shards]
    rows = shards[0].shape[0]
    slots = gather_slots(jnp.concatenate(shards, axis=0) if len(shards) > 1 else shards[0])
    return [
        jnp.concatenate([slot[n * rows : (n + 1) * rows] for slot in slots], axis=0)
        for n in range(len(shards))
    ]


def scatter_sum(partial_sums, rows, pieces=()):
    pieces, given = list(pieces), ()

    def work(gate, *arrived):
        nonlocal given
        if not pieces:
            return arrived
        given = pieces.pop(0)(gate, given)
        arrived, given = lax.optimization_barrier((arrived, given))
        return arrived

    if not short_ring():
        done = lax.psum_scatter(partial_sums, "tp", scatter_dimension=0, tiled=True)
        while pieces:
            work(partial_sums)
        return done, given
    inner = flip_size()
    ring = lax.axis_size("tp") // inner
    slot = lambda number: partial_sums[number * rows : (number + 1) * rows]
    arrived = [None] * ring
    if inner == 2:
        arrived = [flip(slot(ring + (k + 1) % ring)) for k in range(ring)]
        (arrived[0],) = work(partial_sums, arrived[0])
    carried = None
    for k in range(ring):
        total = slot((k + 1) % ring).astype(jnp.float32)
        if arrived[k] is not None:
            total = total + arrived[k].astype(jnp.float32)
        if carried is not None:
            total = total + carried.astype(jnp.float32)
        carried = total.astype(jnp.bfloat16)
        if k < ring - 1:
            (carried,) = work(carried, step_up(carried))
    while pieces:
        work(carried)
    return carried, given


def dot_tn(left, right):
    return lax.dot_general(
        left, right, (((0,), (0,)), ((), ())), preferred_element_type=jnp.float32
    )


def dot_nt(left, right):
    return lax.dot_general(
        left, right, (((1,), (1,)), ((), ())), preferred_element_type=jnp.float32
    )


def mean_of(own, other):
    return ((own.astype(jnp.float32) + other.astype(jnp.float32)) * 0.5).astype(jnp.bfloat16)


def activations(tokens, upstream, w_in, w_out, scale_in, scale_out):
    preact = jnp.dot(tokens, w_in, preferred_element_type=jnp.float32) * scale_in
    value, slope = gelu_parts(preact)
    back = dot_nt(upstream, w_out) * scale_out
    return value.astype(jnp.bfloat16), (back * slope).astype(jnp.bfloat16)


def forward_kernel(*refs, slots, scale_in, scale_out):
    tok_slots, up_slots = refs[:slots], refs[slots : 2 * slots]
    w_in_ref, w_out_ref, hidden_ref, dpre_ref, part_ref, tok_ref, up_ref, acc_ref = refs[2 * slots :]
    step = pl.program_id(0)

    @pl.when(step == 0)
    def _():
        for whole, parts in ((tok_ref, tok_slots), (up_ref, up_slots)):
            rows = parts[0].shape[0]
            for number, part in enumerate(parts):
                whole[number * rows : (number + 1) * rows, :] = part[...]

    preact = jnp.dot(tok_ref[...], w_in_ref[...], preferred_element_type=jnp.float32) * scale_in
    back = dot_nt(up_ref[...], w_out_ref[...]) * scale_out
    value, slope = gelu_parts(preact)
    hidden_ref[...] = value.astype(jnp.bfloat16)
    dpre = (back * slope).astype(jnp.bfloat16)
    dpre_ref[...] = dpre
    part = dot_nt(dpre, w_in_ref[...])

    @pl.when(step == 0)
    def _():
        acc_ref[...] = part

    @pl.when(step > 0)
    def _():
        acc_ref[...] += part

    @pl.when(step == pl.num_programs(0) - 1)
    def _():
        part_ref[...] = (acc_ref[...] * scale_in).astype(jnp.bfloat16)


def forward(tok_slots, up_slots, w_in, w_out, scale_in, scale_out):
    width, hid = w_in.shape
    slots, part_rows = len(tok_slots), tok_slots[0].shape[0]
    rows, cols = slots * part_rows, 256
    if rows > 256 or hid % cols:
        tokens, upstream = jnp.concatenate(tok_slots, axis=0), jnp.concatenate(up_slots, axis=0)
        hidden, dpre = activations(tokens, upstream, w_in, w_out, scale_in, scale_out)
        partials = (dot_nt(dpre, w_in) * scale_in).astype(jnp.bfloat16)
        return hidden, dpre, partials, tokens, upstream
    once = lambda count: pl.BlockSpec((count, width), lambda i: (0, 0), pipeline_mode=pl.Buffered(1))
    block = pl.BlockSpec((rows, cols), lambda i: (0, i))
    wide = jax.ShapeDtypeStruct((rows, width), jnp.bfloat16)
    tall = jax.ShapeDtypeStruct((rows, hid), jnp.bfloat16)
    return pl.pallas_call(
        partial(forward_kernel, slots=slots, scale_in=scale_in, scale_out=scale_out),
        grid=(hid // cols,),
        in_specs=[
            *[once(part_rows)] * (2 * slots),
            pl.BlockSpec((width, cols), lambda i: (0, i)),
            pl.BlockSpec((cols, width), lambda i: (i, 0)),
        ],
        out_specs=[block, block, *[once(rows)] * 3],
        out_shape=[tall, tall, wide, wide, wide],
        scratch_shapes=[pltpu.VMEM((rows, width), jnp.float32)],
        compiler_params=pltpu.CompilerParams(vmem_limit_bytes=52 << 20),
        cost_estimate=pl.CostEstimate(
            flops=6 * rows * width * hid, bytes_accessed=4 * width * hid, transcendentals=2 * rows * hid
        ),
        name="forward",
    )(*tok_slots, *up_slots, w_in, w_out)


def finish_kernel(factor_ref, own_ref, other_ref, left_ref, left2_ref, right_ref, right2_ref, *out_refs):
    grad = dot_tn(left_ref[...], right_ref[...]) + dot_tn(left2_ref[...], right2_ref[...])
    both = own_ref[...].astype(jnp.float32) + other_ref[...].astype(jnp.float32)
    out_refs[-1][...] = (0.5 * both - factor_ref[0] * grad).astype(jnp.bfloat16)


def block_rows(count, width):
    size = 128
    while size * 2 * width <= 1600 << 10 and size < 1024 and count % (size * 2) == 0:
        size *= 2
    return size


def finish(own, other, lefts, rights, factor, start, stop, into=None):
    depth, width = rights[0].shape
    size = block_rows(stop - start, width)
    first = start // size
    tile = pl.BlockSpec((size, width), lambda i: (first + i, 0))
    left = pl.BlockSpec((depth, size), lambda i: (0, first + i))
    right = pl.BlockSpec((depth, width), lambda i: (0, 0), pipeline_mode=pl.Buffered(1))
    operands = [factor.reshape(1), own, other, *lefts, *rights]
    specs = [pl.BlockSpec(memory_space=pltpu.SMEM), tile, tile, left, left, right, right]
    aliases = {}
    if into is not None:
        aliases = {len(operands): 0}
        operands.append(into)
        specs.append(pl.BlockSpec(memory_space=pl.ANY))
    return pl.pallas_call(
        finish_kernel,
        grid=((stop - start) // size,),
        in_specs=specs,
        out_specs=tile,
        out_shape=jax.ShapeDtypeStruct(own.shape, jnp.bfloat16),
        input_output_aliases=aliases,
        compiler_params=pltpu.CompilerParams(vmem_limit_bytes=48 << 20),
        cost_estimate=pl.CostEstimate(
            flops=4 * depth * width * (stop - start),
            bytes_accessed=6 * width * (stop - start),
            transcendentals=0,
        ),
        name="finish",
    )(*operands)


def gather_both(tok, cot):
    if not short_ring():
        slots = [[lax.all_gather(shard, "tp", axis=0, tiled=True)] for shard in (tok, cot)]
        return (*slots, (tok, cot))
    inner = flip_size()
    ring = lax.axis_size("tp") // inner
    current = [tok, cot]
    straight, flipped = [[], []], [[], []]
    for step in range(ring):
        for n in range(2):
            if step:
                held = current[n]
                if step > 1 and inner == 2:
                    held = after(held, flipped[n][step - 2])
                current[n] = step_up(held)
            straight[n].append(current[n])
        for n in range(2):
            if inner == 2:
                held = after(current[n], flipped[n][-1]) if flipped[n] else current[n]
                flipped[n].append(flip(held))
    last = tuple(f[-1] for f in flipped) if inner == 2 else tuple(current)
    return straight[0] + flipped[0], straight[1] + flipped[1], last


def near(tok, cot, w_in, w_out, rate, scale_in, scale_out, bit):
    rows = tok.shape[0]
    other_in = from_partner(w_in, bit)
    tok_slots, up_slots, last = gather_both(tok, cot)
    other_out = from_partner(after(w_out, *last), bit)
    hidden, dpre, partials, tokens, upstream = forward(
        tok_slots, up_slots, w_in, w_out, scale_in, scale_out
    )
    other_tok = from_partner(tokens, bit)
    other_up = from_partner(upstream, bit)
    other_hidden = from_partner(hidden, bit)
    other_dpre = from_partner(dpre, bit)
    factor_in, factor_out = 0.5 * rate * scale_in, 0.5 * rate * scale_out
    sides = [
        (w_in, other_in, (tokens, other_tok), (dpre, other_dpre), factor_in),
        (w_out, other_out, (hidden, other_hidden), (upstream, other_up), factor_out),
    ]

    def piece(side, start, stop, continues):
        def run(gate, given):
            own, other, lefts, rights, factor = sides[side]
            factor = after(factor, gate)
            if continues:
                return (*given[:-1], finish(own, other, lefts, rights, factor, start, stop, given[-1]))
            return (*given, finish(own, other, lefts, rights, factor, start, stop))

        return run

    pieces = []
    for side in range(2):
        count = sides[side][0].shape[0]
        half = count // 256 * 128
        pieces += [piece(side, 0, half, False), piece(side, half, count, True)]
    input_grad, (mixed_in, mixed_out) = scatter_sum(partials, rows, pieces)
    return input_grad, mixed_in, mixed_out


def update_kernel(factor_ref, own_ref, left_ref, right_ref, *out_refs, cuts):
    for out_ref, (lo, hi) in zip(out_refs, cuts):
        grad = dot_tn(left_ref[...], right_ref[:, lo:hi])
        out_ref[...] = (own_ref[:, lo:hi].astype(jnp.float32) - factor_ref[0] * grad).astype(jnp.bfloat16)


def update(own, left, right, factor, cuts):
    depth, width = right.shape
    count = own.shape[0]
    size = block_rows(count, width)
    return pl.pallas_call(
        partial(update_kernel, cuts=cuts),
        grid=(count // size,),
        in_specs=[
            pl.BlockSpec(memory_space=pltpu.SMEM),
            pl.BlockSpec((size, width), lambda i: (i, 0)),
            pl.BlockSpec((depth, size), lambda i: (0, i)),
            pl.BlockSpec((depth, width), lambda i: (0, 0), pipeline_mode=pl.Buffered(1)),
        ],
        out_specs=[pl.BlockSpec((size, hi - lo), lambda i: (i, 0)) for lo, hi in cuts],
        out_shape=[jax.ShapeDtypeStruct((count, hi - lo), jnp.bfloat16) for lo, hi in cuts],
        compiler_params=pltpu.CompilerParams(vmem_limit_bytes=48 << 20),
        cost_estimate=pl.CostEstimate(
            flops=2 * depth * width * count, bytes_accessed=4 * width * count, transcendentals=0
        ),
        name="update",
    )(factor.reshape(1), own, left, right)


def far(tok, cot, w_in, w_out, rate, scale_in, scale_out, bit):
    rows = tok.shape[0]
    unit = 128
    units = w_out.shape[0] // unit
    tok_other = from_partner(tok, bit)
    other_in = from_partner(w_in, bit)
    sent = [tok_other, other_in]

    def send(value):
        sent.append(from_partner(after(value, sent[-2]), bit))
        return sent[-1]

    tok_slots, up_slots, _ = gather_both(tok, cot)
    hidden, dpre, partials, tokens, upstream = forward(
        tok_slots, up_slots, w_in, w_out, scale_in, scale_out
    )
    dpre_other = from_partner(after(dpre, tok_other), bit)
    (new_out,) = update(w_out, hidden, upstream, rate * scale_out, ((0, w_out.shape[1]),))
    input_grad, _ = scatter_sum(after(partials, new_out), rows)
    tokens_other = gather_rows(after(tok_other, input_grad))[0]
    marks = [0, units // 4, units // 2, 3 * units // 4, units - 1, units]
    cuts = [(lo * unit, hi * unit) for lo, hi in zip(marks, marks[1:]) if lo < hi]
    mixed_in, mixed_out = None, jnp.zeros_like(w_out)
    for number, (lo, hi) in enumerate(cuts):
        own = new_out[lo:hi]
        other = send(own)
        mixed_out = lax.dynamic_update_slice(mixed_out, mean_of(own, other), (lo, 0))
        if number == 0:
            factor = after(0.5 * rate * scale_in, other)
            mixed_in = finish(
                w_in, other_in, (tokens, tokens_other), (dpre, dpre_other), factor, 0, w_in.shape[0]
            )
    return input_grad, mixed_in, mixed_out


def per_device(tokens, cotangent, w_in, w_out, gossip_step):
    width = tokens.shape[2]
    hid_dev = w_in.shape[2]
    scale_in = 1.0 / width**0.5
    scale_out = 1.0 / (hid_dev * lax.axis_size("tp")) ** 0.5
    rate = 16.0 / (8.0 + gossip_step[0].astype(jnp.float32))
    nbits = lax.axis_size("rep").bit_length() - 1
    branches = [
        partial(near if bit == 0 else far, scale_in=scale_in, scale_out=scale_out, bit=bit)
        for bit in range(nbits)
    ]
    input_grad, mixed_in, mixed_out = lax.switch(
        gossip_step[0] % nbits, branches, tokens[0], cotangent[0], w_in[0], w_out[0], rate
    )
    return (input_grad[None], mixed_in[None], mixed_out[None])


def solution(mesh):
    return jax.shard_map(
        per_device,
        mesh=mesh,
        in_specs=(
            P("rep", "tp", None),
            P("rep", "tp", None),
            P("rep", None, "tp"),
            P("rep", "tp", None),
            P(),
        ),
        out_specs=(P("rep", "tp", None), P("rep", None, "tp"), P("rep", "tp", None)),
        check_vma=False,
    )
```

```python
from functools import partial

import jax
import jax.numpy as jnp
from jax import lax
from jax.experimental import pallas as pl
from jax.experimental.pallas import tpu as pltpu
from jax.sharding import PartitionSpec as P


def from_partner(value, stride):
    mask = 2**stride
    pairs = [(source, source ^ mask) for source in range(lax.axis_size("rep"))]
    return lax.ppermute(value, "rep", pairs)


def after(value, *earlier):
    return lax.optimization_barrier((value, *earlier))[0]


def gelu_parts(preact):
    cdf = 0.5 * (1.0 + lax.erf(preact * 0.7071067811865476))
    dens = jnp.exp(-0.5 * preact * preact) * 0.3989422804014327
    return (preact * cdf, cdf + preact * dens)


def flip_size():
    return 2 if lax.axis_size("tp") % 2 == 0 else 1


def step_up(value):
    size, inner = lax.axis_size("tp"), flip_size()
    return lax.ppermute(value, "tp", [(i, (i + inner) % size) for i in range(size)])


def step_down(value):
    size, inner = lax.axis_size("tp"), flip_size()
    return lax.ppermute(value, "tp", [(i, (i - inner) % size) for i in range(size)])


def flip(value):
    return lax.ppermute(value, "tp", [(i, i ^ 1) for i in range(lax.axis_size("tp"))])


def short_ring():
    return lax.axis_size("tp") // flip_size() <= 4


def gather_slots(shard):
    inner = flip_size()
    ring = lax.axis_size("tp") // inner
    straight, flipped, current = [], [], shard
    for step in range(ring):
        if step:
            current = step_up(current)
        straight.append(current)
        if inner == 2:
            flipped.append(flip(current))
    return straight + flipped


def gather_rows(*shards):
    if not short_ring():
        return [lax.all_gather(shard, "tp", axis=0, tiled=True) for shard in shards]
    rows = shards[0].shape[0]
    slots = gather_slots(jnp.concatenate(shards, axis=0) if len(shards) > 1 else shards[0])
    return [
        jnp.concatenate([slot[n * rows : (n + 1) * rows] for slot in slots], axis=0)
        for n in range(len(shards))
    ]


def scatter_sum(partial_sums, rows, pieces=()):
    pieces, given = list(pieces), ()

    def work(gate, *arrived):
        nonlocal given
        if not pieces:
            return arrived
        given = pieces.pop(0)(gate, given)
        arrived, given = lax.optimization_barrier((arrived, given))
        return arrived

    if not short_ring():
        done = lax.psum_scatter(partial_sums, "tp", scatter_dimension=0, tiled=True)
        while pieces:
            work(partial_sums)
        return done, given
    inner = flip_size()
    size = lax.axis_size("tp")
    ring = size // inner
    slot = lambda number: partial_sums[number * rows : (number + 1) * rows]
    sums = [slot(k).astype(jnp.float32) for k in range(ring)]
    if inner == 2:
        (arrived,) = work(partial_sums, flip(partial_sums[ring * rows :]))
        arrived = arrived.astype(jnp.float32).reshape(ring, rows, -1)
        sums = [own + arrived[k] for k, own in enumerate(sums)]
    leaving = [total.astype(jnp.bfloat16) for total in sums[1:]]
    arrived = [
        lax.ppermute(value, "tp", [(i, (i - k * inner) % size) for i in range(size)])
        for k, value in enumerate(leaving, 1)
    ]
    total = sums[0]
    if leaving:
        arrived = work(leaving[0], *arrived)
    for other in arrived:
        total = total + other.astype(jnp.float32)
    carried = total.astype(jnp.bfloat16)
    while pieces:
        work(carried)
    return carried, given


def dot_tn(left, right):
    return lax.dot_general(
        left, right, (((0,), (0,)), ((), ())), preferred_element_type=jnp.float32
    )


def dot_nt(left, right):
    return lax.dot_general(
        left, right, (((1,), (1,)), ((), ())), preferred_element_type=jnp.float32
    )


def mean_of(own, other):
    return ((own.astype(jnp.float32) + other.astype(jnp.float32)) * 0.5).astype(jnp.bfloat16)


def activations(tokens, upstream, w_in, w_out, scale_in, scale_out):
    preact = jnp.dot(tokens, w_in, preferred_element_type=jnp.float32) * scale_in
    value, slope = gelu_parts(preact)
    back = dot_nt(upstream, w_out) * scale_out
    return value.astype(jnp.bfloat16), (back * slope).astype(jnp.bfloat16)


def forward_kernel(*refs, slots, scale_in, scale_out):
    tok_slots, up_slots = refs[:slots], refs[slots : 2 * slots]
    w_in_ref, w_out_ref, both_ref, sides_out, tok_ref, up_ref, sems = refs[2 * slots :]
    step = pl.program_id(0)
    copies = [
        pltpu.make_async_copy(tok_ref, sides_out.at[0], sems.at[0]),
        pltpu.make_async_copy(up_ref, sides_out.at[1], sems.at[1]),
    ]

    @pl.when(step == 0)
    def _():
        for whole, parts, copy in zip((tok_ref, up_ref), (tok_slots, up_slots), copies):
            rows = parts[0].shape[0]
            for number, part in enumerate(parts):
                whole[number * rows : (number + 1) * rows, :] = part[...]
            copy.start()

    preact = jnp.dot(tok_ref[...], w_in_ref[...], preferred_element_type=jnp.float32) * scale_in
    back = dot_nt(up_ref[...], w_out_ref[...]) * scale_out
    value, slope = gelu_parts(preact)
    both_ref[0] = value.astype(jnp.bfloat16)
    both_ref[1] = (back * slope).astype(jnp.bfloat16)

    @pl.when(step == pl.num_programs(0) - 1)
    def _():
        for copy in copies:
            copy.wait()


def forward(tok_slots, up_slots, w_in, w_out, scale_in, scale_out):
    width, hid = w_in.shape
    slots, part_rows = len(tok_slots), tok_slots[0].shape[0]
    rows, cols = slots * part_rows, 256
    if rows > 256 or hid % cols:
        tokens, upstream = jnp.concatenate(tok_slots, axis=0), jnp.concatenate(up_slots, axis=0)
        both = activations(tokens, upstream, w_in, w_out, scale_in, scale_out)
        return jnp.stack(both), jnp.stack([tokens, upstream])
    once = pl.BlockSpec((part_rows, width), lambda i: (0, 0), pipeline_mode=pl.Buffered(1))
    return pl.pallas_call(
        partial(forward_kernel, slots=slots, scale_in=scale_in, scale_out=scale_out),
        grid=(hid // cols,),
        in_specs=[
            *[once] * (2 * slots),
            pl.BlockSpec((width, cols), lambda i: (0, i)),
            pl.BlockSpec((cols, width), lambda i: (i, 0)),
        ],
        out_specs=[
            pl.BlockSpec((2, rows, cols), lambda i: (0, 0, i)),
            pl.BlockSpec(memory_space=pl.ANY),
        ],
        out_shape=[
            jax.ShapeDtypeStruct((2, rows, hid), jnp.bfloat16),
            jax.ShapeDtypeStruct((2, rows, width), jnp.bfloat16),
        ],
        scratch_shapes=[
            pltpu.VMEM((rows, width), jnp.bfloat16),
            pltpu.VMEM((rows, width), jnp.bfloat16),
            pltpu.SemaphoreType.DMA((2,)),
        ],
        compiler_params=pltpu.CompilerParams(vmem_limit_bytes=48 << 20),
        cost_estimate=pl.CostEstimate(
            flops=4 * rows * width * hid, bytes_accessed=4 * width * hid, transcendentals=2 * rows * hid
        ),
        name="forward",
    )(*tok_slots, *up_slots, w_in, w_out)


def finish_kernel(factor_ref, own_ref, other_ref, left_ref, left2_ref, right_ref, right2_ref, out_ref):
    grad = dot_tn(left_ref[...], right_ref[...]) + dot_tn(left2_ref[...], right2_ref[...])
    both = own_ref[...].astype(jnp.float32) + other_ref[...].astype(jnp.float32)
    out_ref[...] = (0.5 * both - factor_ref[0] * grad).astype(jnp.bfloat16)


def block_rows(count, width):
    size = 128
    while size * 2 * width <= 1600 << 10 and size < 1024 and count % (size * 2) == 0:
        size *= 2
    return size


def finish(own, other, lefts, rights, factor):
    depth, width = rights[0][0].shape[1:]
    count = own.shape[0]
    size = block_rows(count, width)
    tile = pl.BlockSpec((size, width), lambda i: (i, 0))
    left = lambda place: pl.BlockSpec((None, depth, size), lambda i: (place, 0, i))
    right = lambda place: pl.BlockSpec(
        (None, depth, width), lambda i: (place, 0, 0), pipeline_mode=pl.Buffered(1)
    )
    return pl.pallas_call(
        finish_kernel,
        grid=(count // size,),
        in_specs=[
            pl.BlockSpec(memory_space=pltpu.SMEM),
            tile,
            tile,
            *[left(place) for _, place in lefts],
            *[right(place) for _, place in rights],
        ],
        out_specs=tile,
        out_shape=jax.ShapeDtypeStruct(own.shape, jnp.bfloat16),
        compiler_params=pltpu.CompilerParams(vmem_limit_bytes=48 << 20),
        cost_estimate=pl.CostEstimate(
            flops=4 * depth * width * count, bytes_accessed=6 * width * count, transcendentals=0
        ),
        name="finish",
    )(factor.reshape(1), own, other, *[array for array, _ in lefts + rights])


def gather_both(tok, cot):
    if not short_ring():
        return [[lax.all_gather(shard, "tp", axis=0, tiled=True)] for shard in (tok, cot)]
    inner = flip_size()
    ring = lax.axis_size("tp") // inner
    current = [tok, cot]
    straight, flipped = [[], []], [[], []]
    for step in range(ring):
        for n in range(2):
            if step:
                held = current[n]
                if step > 1 and inner == 2:
                    held = after(held, flipped[n][step - 2])
                current[n] = step_up(held)
            straight[n].append(current[n])
        for n in range(2):
            if inner == 2 and n == 1 and ring > 2 and step == ring - 1:
                flipped[n].append(step_down(after(flipped[n][0], straight[n][-2])))
            elif inner == 2:
                held = after(current[n], flipped[n][-1]) if flipped[n] else current[n]
                flipped[n].append(flip(held))
    return straight[0] + flipped[0], straight[1] + flipped[1]


def near(tok, cot, w_in, w_out, rate, scale_in, scale_out, bit):
    rows = tok.shape[0]
    other_in = from_partner(w_in, bit)
    tok_slots, up_slots = gather_both(tok, cot)
    up_slots = [after(up_slots[0], other_in), *up_slots[1:]]
    both, sides = forward(tok_slots, up_slots, w_in, w_out, scale_in, scale_out)
    other_both = from_partner(both, bit)
    other_sides = from_partner(sides, bit)
    partials = (dot_nt(both[1], w_in) * scale_in).astype(jnp.bfloat16)
    other_out = from_partner(after(w_out, other_both, other_sides, partials), bit)
    stacks = [
        (w_in, other_in, ((sides, 0), (other_sides, 0)), ((both, 1), (other_both, 1)), 0.5 * rate * scale_in),
        (w_out, other_out, ((both, 0), (other_both, 0)), ((sides, 1), (other_sides, 1)), 0.5 * rate * scale_out),
    ]

    def piece(own, other, lefts, rights, factor):
        def run(gate, given):
            return (*given, finish(own, other, lefts, rights, after(factor, gate)))

        return run

    pieces = [piece(*stack) for stack in stacks]
    input_grad, (mixed_in, mixed_out) = scatter_sum(partials, rows, pieces)
    return input_grad, mixed_in, mixed_out


def update_kernel(factor_ref, own_ref, left_ref, right_ref, *out_refs, cuts):
    for out_ref, (lo, hi) in zip(out_refs, cuts):
        grad = dot_tn(left_ref[...], right_ref[:, lo:hi])
        out_ref[...] = (own_ref[:, lo:hi].astype(jnp.float32) - factor_ref[0] * grad).astype(jnp.bfloat16)


def update(own, left, right, factor, cuts):
    depth, width = right.shape
    count = own.shape[0]
    size = block_rows(count, width)
    return pl.pallas_call(
        partial(update_kernel, cuts=cuts),
        grid=(count // size,),
        in_specs=[
            pl.BlockSpec(memory_space=pltpu.SMEM),
            pl.BlockSpec((size, width), lambda i: (i, 0)),
            pl.BlockSpec((depth, size), lambda i: (0, i)),
            pl.BlockSpec((depth, width), lambda i: (0, 0), pipeline_mode=pl.Buffered(1)),
        ],
        out_specs=[pl.BlockSpec((size, hi - lo), lambda i: (i, 0)) for lo, hi in cuts],
        out_shape=[jax.ShapeDtypeStruct((count, hi - lo), jnp.bfloat16) for lo, hi in cuts],
        compiler_params=pltpu.CompilerParams(vmem_limit_bytes=48 << 20),
        cost_estimate=pl.CostEstimate(
            flops=2 * depth * width * count, bytes_accessed=4 * width * count, transcendentals=0
        ),
        name="update",
    )(factor.reshape(1), own, left, right)


def far(tok, cot, w_in, w_out, rate, scale_in, scale_out, bit):
    rows = tok.shape[0]
    unit = 128
    units = w_out.shape[0] // unit
    tok_other = from_partner(tok, bit)
    other_in = from_partner(w_in, bit)
    sent = [tok_other, other_in]

    def send(value):
        sent.append(from_partner(after(value, sent[-2]), bit))
        return sent[-1]

    tok_slots, up_slots = gather_both(tok, cot)
    both, sides = forward(tok_slots, up_slots, w_in, w_out, scale_in, scale_out)
    dpre = both[1]
    dpre_other = from_partner(after(dpre, tok_other), bit)
    (new_out,) = update(w_out, both[0], sides[1], rate * scale_out, ((0, w_out.shape[1]),))
    partials = (dot_nt(after(dpre, new_out), w_in) * scale_in).astype(jnp.bfloat16)
    input_grad, _ = scatter_sum(partials, rows)
    tokens_other = gather_rows(after(tok_other, input_grad))[0]
    marks = [0, units // 4, units // 2, 3 * units // 4, units - 1, units]
    cuts = [(lo * unit, hi * unit) for lo, hi in zip(marks, marks[1:]) if lo < hi]
    mixed_in, mixed_out = None, jnp.zeros_like(w_out)
    for number, (lo, hi) in enumerate(cuts):
        own = new_out[lo:hi]
        other = send(own)
        mixed_out = lax.dynamic_update_slice(mixed_out, mean_of(own, other), (lo, 0))
        if number == 0:
            factor = after(0.5 * rate * scale_in, other)
            lefts = ((sides, 0), (tokens_other[None], 0))
            rights = ((both, 1), (dpre_other[None], 0))
            mixed_in = finish(w_in, other_in, lefts, rights, factor)
    return input_grad, mixed_in, mixed_out


def per_device(tokens, cotangent, w_in, w_out, gossip_step):
    width = tokens.shape[2]
    hid_dev = w_in.shape[2]
    scale_in = 1.0 / width**0.5
    scale_out = 1.0 / (hid_dev * lax.axis_size("tp")) ** 0.5
    rate = 16.0 / (8.0 + gossip_step[0].astype(jnp.float32))
    nbits = lax.axis_size("rep").bit_length() - 1
    branches = [
        partial(near if bit == 0 else far, scale_in=scale_in, scale_out=scale_out, bit=bit)
        for bit in range(nbits)
    ]
    input_grad, mixed_in, mixed_out = lax.switch(
        gossip_step[0] % nbits, branches, tokens[0], cotangent[0], w_in[0], w_out[0], rate
    )
    return (input_grad[None], mixed_in[None], mixed_out[None])


def solution(mesh):
    return jax.shard_map(
        per_device,
        mesh=mesh,
        in_specs=(
            P("rep", "tp", None),
            P("rep", "tp", None),
            P("rep", None, "tp"),
            P("rep", "tp", None),
            P(),
        ),
        out_specs=(P("rep", "tp", None), P("rep", None, "tp"), P("rep", "tp", None)),
        check_vma=False,
    )
```

```python
from functools import partial

import jax
import jax.numpy as jnp
from jax import lax
from jax.experimental import pallas as pl
from jax.experimental.pallas import tpu as pltpu
from jax.sharding import PartitionSpec as P


def from_partner(value, stride):
    mask = 2**stride
    pairs = [(source, source ^ mask) for source in range(lax.axis_size("rep"))]
    return lax.ppermute(value, "rep", pairs)


def after(value, *earlier):
    return lax.optimization_barrier((value, *earlier))[0]


def gelu_parts(preact):
    cdf = 0.5 * (1.0 + lax.erf(preact * 0.7071067811865476))
    dens = jnp.exp(-0.5 * preact * preact) * 0.3989422804014327
    return (preact * cdf, cdf + preact * dens)


def flip_size():
    return 2 if lax.axis_size("tp") % 2 == 0 else 1


def step_up(value):
    size, inner = lax.axis_size("tp"), flip_size()
    return lax.ppermute(value, "tp", [(i, (i + inner) % size) for i in range(size)])


def step_down(value):
    size, inner = lax.axis_size("tp"), flip_size()
    return lax.ppermute(value, "tp", [(i, (i - inner) % size) for i in range(size)])


def flip(value):
    return lax.ppermute(value, "tp", [(i, i ^ 1) for i in range(lax.axis_size("tp"))])


def short_ring():
    return lax.axis_size("tp") // flip_size() <= 4


def gather_slots(shard):
    inner = flip_size()
    ring = lax.axis_size("tp") // inner
    straight, flipped, current = [], [], shard
    for step in range(ring):
        if step:
            current = step_up(current)
        straight.append(current)
        if inner == 2:
            flipped.append(flip(current))
    return straight + flipped


def gather_rows(*shards):
    if not short_ring():
        return [lax.all_gather(shard, "tp", axis=0, tiled=True) for shard in shards]
    rows = shards[0].shape[0]
    slots = gather_slots(jnp.concatenate(shards, axis=0) if len(shards) > 1 else shards[0])
    return [
        jnp.concatenate([slot[n * rows : (n + 1) * rows] for slot in slots], axis=0)
        for n in range(len(shards))
    ]


def scatter_sum(halves, rows, pieces=()):
    pieces, given = list(pieces), ()

    def work(gate, *arrived):
        nonlocal given
        if not pieces:
            return arrived
        given = pieces.pop(0)(gate, given)
        arrived, given = lax.optimization_barrier((arrived, given))
        return arrived

    if not short_ring():
        whole = jnp.concatenate(halves, axis=0)
        done = lax.psum_scatter(whole, "tp", scatter_dimension=0, tiled=True)
        while pieces:
            work(halves[0])
        return done, given
    inner = flip_size()
    size = lax.axis_size("tp")
    ring = size // inner
    straight = halves[0] if inner == 2 else jnp.concatenate(halves, axis=0)
    slot = lambda number: straight[number * rows : (number + 1) * rows]
    sums = [slot(k).astype(jnp.float32) for k in range(ring)]
    if inner == 2:
        (arrived,) = work(halves[0], flip(halves[1]))
        sums = [
            own + arrived[k * rows : (k + 1) * rows].astype(jnp.float32) for k, own in enumerate(sums)
        ]
    leaving = [total.astype(jnp.bfloat16) for total in sums[1:]]
    arrived = [
        lax.ppermute(value, "tp", [(i, (i - k * inner) % size) for i in range(size)])
        for k, value in enumerate(leaving, 1)
    ]
    total = sums[0]
    if leaving:
        arrived = work(leaving[0], *arrived)
    for other in arrived:
        total = total + other.astype(jnp.float32)
    carried = total.astype(jnp.bfloat16)
    while pieces:
        work(carried)
    return carried, given


def dot_tn(left, right):
    return lax.dot_general(
        left, right, (((0,), (0,)), ((), ())), preferred_element_type=jnp.float32
    )


def dot_nt(left, right):
    return lax.dot_general(
        left, right, (((1,), (1,)), ((), ())), preferred_element_type=jnp.float32
    )


def mean_of(own, other):
    return ((own.astype(jnp.float32) + other.astype(jnp.float32)) * 0.5).astype(jnp.bfloat16)


def activations(tokens, upstream, w_in, w_out, scale_in, scale_out):
    preact = jnp.dot(tokens, w_in, preferred_element_type=jnp.float32) * scale_in
    value, slope = gelu_parts(preact)
    back = dot_nt(upstream, w_out) * scale_out
    return value.astype(jnp.bfloat16), (back * slope).astype(jnp.bfloat16)


def forward_kernel(*refs, slots, scale_in, scale_out):
    tok_slots, up_slots = refs[:slots], refs[slots : 2 * slots]
    w_in_ref, w_out_ref, both_ref, sides_out, tok_ref, up_ref, sems = refs[2 * slots :]
    step = pl.program_id(0)
    copies = [
        pltpu.make_async_copy(tok_ref, sides_out.at[0], sems.at[0]),
        pltpu.make_async_copy(up_ref, sides_out.at[1], sems.at[1]),
    ]

    @pl.when(step == 0)
    def _():
        for whole, parts, copy in zip((tok_ref, up_ref), (tok_slots, up_slots), copies):
            rows = parts[0].shape[0]
            for number, part in enumerate(parts):
                whole[number * rows : (number + 1) * rows, :] = part[...]
            copy.start()

    preact = jnp.dot(tok_ref[...], w_in_ref[...], preferred_element_type=jnp.float32) * scale_in
    back = dot_nt(up_ref[...], w_out_ref[...]) * scale_out
    value, slope = gelu_parts(preact)
    both_ref[0] = value.astype(jnp.bfloat16)
    both_ref[1] = (back * slope).astype(jnp.bfloat16)

    @pl.when(step == pl.num_programs(0) - 1)
    def _():
        for copy in copies:
            copy.wait()


def forward(tok_slots, up_slots, w_in, w_out, scale_in, scale_out):
    width, hid = w_in.shape
    slots, part_rows = len(tok_slots), tok_slots[0].shape[0]
    rows, cols = slots * part_rows, 256
    if rows > 256 or hid % cols:
        tokens, upstream = jnp.concatenate(tok_slots, axis=0), jnp.concatenate(up_slots, axis=0)
        both = activations(tokens, upstream, w_in, w_out, scale_in, scale_out)
        return jnp.stack(both), jnp.stack([tokens, upstream])
    once = pl.BlockSpec((part_rows, width), lambda i: (0, 0), pipeline_mode=pl.Buffered(1))
    return pl.pallas_call(
        partial(forward_kernel, slots=slots, scale_in=scale_in, scale_out=scale_out),
        grid=(hid // cols,),
        in_specs=[
            *[once] * (2 * slots),
            pl.BlockSpec((width, cols), lambda i: (0, i)),
            pl.BlockSpec((cols, width), lambda i: (i, 0)),
        ],
        out_specs=[
            pl.BlockSpec((2, rows, cols), lambda i: (0, 0, i)),
            pl.BlockSpec(memory_space=pl.ANY),
        ],
        out_shape=[
            jax.ShapeDtypeStruct((2, rows, hid), jnp.bfloat16),
            jax.ShapeDtypeStruct((2, rows, width), jnp.bfloat16),
        ],
        scratch_shapes=[
            pltpu.VMEM((rows, width), jnp.bfloat16),
            pltpu.VMEM((rows, width), jnp.bfloat16),
            pltpu.SemaphoreType.DMA((2,)),
        ],
        compiler_params=pltpu.CompilerParams(vmem_limit_bytes=48 << 20),
        cost_estimate=pl.CostEstimate(
            flops=4 * rows * width * hid, bytes_accessed=4 * width * hid, transcendentals=2 * rows * hid
        ),
        name="forward",
    )(*tok_slots, *up_slots, w_in, w_out)


def partial_kernel(dpre_ref, w_in_ref, first_ref, second_ref, *, scale_in):
    sums = (dot_nt(dpre_ref[...], w_in_ref[...]) * scale_in).astype(jnp.bfloat16)
    half = first_ref.shape[0]
    first_ref[...] = sums[:half]
    second_ref[...] = sums[half:]


def partial_sums(both, w_in, scale_in):
    _, rows, hid = both.shape
    width, half, size = w_in.shape[0], rows // 2, 1024
    if rows > 256 or width % size or half % 16:
        whole = (dot_nt(both[1], w_in) * scale_in).astype(jnp.bfloat16)
        return whole[:half], whole[half:]
    part = pl.BlockSpec((half, size), lambda i: (0, i))
    return pl.pallas_call(
        partial(partial_kernel, scale_in=scale_in),
        grid=(width // size,),
        in_specs=[
            pl.BlockSpec((None, rows, hid), lambda i: (1, 0, 0), pipeline_mode=pl.Buffered(1)),
            pl.BlockSpec((size, hid), lambda i: (i, 0)),
        ],
        out_specs=[part, part],
        out_shape=[jax.ShapeDtypeStruct((half, width), jnp.bfloat16)] * 2,
        compiler_params=pltpu.CompilerParams(vmem_limit_bytes=32 << 20),
        cost_estimate=pl.CostEstimate(
            flops=2 * rows * width * hid, bytes_accessed=2 * width * hid, transcendentals=0
        ),
        name="partial_sums",
    )(both, w_in)


def finish_kernel(
    factor_ref, own_ref, other_ref, left_ref, left2_ref, right_ref, right2_ref, out_ref, lefts_ref, rights_ref
):
    depth = left_ref.shape[0]

    @pl.when(pl.program_id(0) == 0)
    def _():
        rights_ref[:depth] = right_ref[...]
        rights_ref[depth:] = right2_ref[...]

    lefts_ref[:depth] = left_ref[...]
    lefts_ref[depth:] = left2_ref[...]
    grad = dot_tn(lefts_ref[...], rights_ref[...])
    both = own_ref[...].astype(jnp.float32) + other_ref[...].astype(jnp.float32)
    out_ref[...] = (0.5 * both - factor_ref[0] * grad).astype(jnp.bfloat16)


def block_rows(count, width):
    size = 128
    while size * 2 * width <= 1600 << 10 and size < 1024 and count % (size * 2) == 0:
        size *= 2
    return size


def finish(own, other, lefts, rights, factor):
    depth, width = rights[0][0].shape[1:]
    count = own.shape[0]
    size = block_rows(count, width)
    tile = pl.BlockSpec((size, width), lambda i: (i, 0))
    left = lambda place: pl.BlockSpec((None, depth, size), lambda i: (place, 0, i))
    right = lambda place: pl.BlockSpec(
        (None, depth, width), lambda i: (place, 0, 0), pipeline_mode=pl.Buffered(1)
    )
    return pl.pallas_call(
        finish_kernel,
        grid=(count // size,),
        in_specs=[
            pl.BlockSpec(memory_space=pltpu.SMEM),
            tile,
            tile,
            *[left(place) for _, place in lefts],
            *[right(place) for _, place in rights],
        ],
        out_specs=tile,
        out_shape=jax.ShapeDtypeStruct(own.shape, jnp.bfloat16),
        scratch_shapes=[
            pltpu.VMEM((2 * depth, size), jnp.bfloat16),
            pltpu.VMEM((2 * depth, width), jnp.bfloat16),
        ],
        compiler_params=pltpu.CompilerParams(vmem_limit_bytes=48 << 20),
        cost_estimate=pl.CostEstimate(
            flops=4 * depth * width * count, bytes_accessed=6 * width * count, transcendentals=0
        ),
        name="finish",
    )(factor.reshape(1), own, other, *[array for array, _ in lefts + rights])


def gather_both(tok, cot):
    if not short_ring():
        return [[lax.all_gather(shard, "tp", axis=0, tiled=True)] for shard in (tok, cot)]
    inner = flip_size()
    ring = lax.axis_size("tp") // inner
    current = [tok, cot]
    straight, flipped = [[], []], [[], []]
    for step in range(ring):
        for n in range(2):
            if step:
                held = current[n]
                if step > 1 and inner == 2:
                    held = after(held, flipped[n][step - 2])
                current[n] = step_up(held)
            straight[n].append(current[n])
        for n in range(2):
            if inner == 2 and n == 1 and ring > 2 and step == ring - 1:
                flipped[n].append(step_down(after(flipped[n][0], straight[n][-2])))
            elif inner == 2:
                held = after(current[n], flipped[n][-1]) if flipped[n] else current[n]
                flipped[n].append(flip(held))
    return straight[0] + flipped[0], straight[1] + flipped[1]


def near(tok, cot, w_in, w_out, rate, scale_in, scale_out, bit):
    rows = tok.shape[0]
    other_in = from_partner(w_in, bit)
    tok_slots, up_slots = gather_both(tok, cot)
    up_slots = [after(up_slots[0], other_in), *up_slots[1:]]
    both, sides = forward(tok_slots, up_slots, w_in, w_out, scale_in, scale_out)
    other_both = from_partner(both, bit)
    other_sides = from_partner(sides, bit)
    partials = partial_sums(both, w_in, scale_in)
    other_out = from_partner(after(w_out, other_both, other_sides, *partials), bit)
    stacks = [
        (w_in, other_in, ((sides, 0), (other_sides, 0)), ((both, 1), (other_both, 1)), 0.5 * rate * scale_in),
        (w_out, other_out, ((both, 0), (other_both, 0)), ((sides, 1), (other_sides, 1)), 0.5 * rate * scale_out),
    ]

    def piece(own, other, lefts, rights, factor):
        def run(gate, given):
            return (*given, finish(own, other, lefts, rights, after(factor, gate)))

        return run

    pieces = [piece(*stack) for stack in stacks]
    input_grad, (mixed_in, mixed_out) = scatter_sum(partials, rows, pieces)
    return input_grad, mixed_in, mixed_out


def update_kernel(factor_ref, own_ref, left_ref, right_ref, *out_refs, cuts):
    for out_ref, (lo, hi) in zip(out_refs, cuts):
        grad = dot_tn(left_ref[...], right_ref[:, lo:hi])
        out_ref[...] = (own_ref[:, lo:hi].astype(jnp.float32) - factor_ref[0] * grad).astype(jnp.bfloat16)


def update(own, left, right, factor, cuts):
    depth, width = right.shape
    count = own.shape[0]
    size = block_rows(count, width)
    return pl.pallas_call(
        partial(update_kernel, cuts=cuts),
        grid=(count // size,),
        in_specs=[
            pl.BlockSpec(memory_space=pltpu.SMEM),
            pl.BlockSpec((size, width), lambda i: (i, 0)),
            pl.BlockSpec((depth, size), lambda i: (0, i)),
            pl.BlockSpec((depth, width), lambda i: (0, 0), pipeline_mode=pl.Buffered(1)),
        ],
        out_specs=[pl.BlockSpec((size, hi - lo), lambda i: (i, 0)) for lo, hi in cuts],
        out_shape=[jax.ShapeDtypeStruct((count, hi - lo), jnp.bfloat16) for lo, hi in cuts],
        compiler_params=pltpu.CompilerParams(vmem_limit_bytes=48 << 20),
        cost_estimate=pl.CostEstimate(
            flops=2 * depth * width * count, bytes_accessed=4 * width * count, transcendentals=0
        ),
        name="update",
    )(factor.reshape(1), own, left, right)


def far(tok, cot, w_in, w_out, rate, scale_in, scale_out, bit):
    rows = tok.shape[0]
    unit = 128
    units = w_out.shape[0] // unit
    tok_other = from_partner(tok, bit)
    other_in = from_partner(w_in, bit)
    sent = [tok_other, other_in]

    def send(value):
        sent.append(from_partner(after(value, sent[-2]), bit))
        return sent[-1]

    tok_slots, up_slots = gather_both(tok, cot)
    both, sides = forward(tok_slots, up_slots, w_in, w_out, scale_in, scale_out)
    dpre = both[1]
    dpre_other = from_partner(after(dpre, tok_other), bit)
    (new_out,) = update(w_out, both[0], sides[1], rate * scale_out, ((0, w_out.shape[1]),))
    partials = partial_sums(after(both, new_out), w_in, scale_in)
    input_grad, _ = scatter_sum(partials, rows)
    tokens_other = gather_rows(after(tok_other, input_grad))[0]
    marks = [0, units // 4, units // 2, 3 * units // 4, units - 1, units]
    cuts = [(lo * unit, hi * unit) for lo, hi in zip(marks, marks[1:]) if lo < hi]
    mixed_in, mixed_out = None, jnp.zeros_like(w_out)
    for number, (lo, hi) in enumerate(cuts):
        own = new_out[lo:hi]
        other = send(own)
        mixed_out = lax.dynamic_update_slice(mixed_out, mean_of(own, other), (lo, 0))
        if number == 0:
            factor = after(0.5 * rate * scale_in, other)
            lefts = ((sides, 0), (tokens_other[None], 0))
            rights = ((both, 1), (dpre_other[None], 0))
            mixed_in = finish(w_in, other_in, lefts, rights, factor)
    return input_grad, mixed_in, mixed_out


def per_device(tokens, cotangent, w_in, w_out, gossip_step):
    width = tokens.shape[2]
    hid_dev = w_in.shape[2]
    scale_in = 1.0 / width**0.5
    scale_out = 1.0 / (hid_dev * lax.axis_size("tp")) ** 0.5
    rate = 16.0 / (8.0 + gossip_step[0].astype(jnp.float32))
    nbits = lax.axis_size("rep").bit_length() - 1
    branches = [
        partial(near if bit == 0 else far, scale_in=scale_in, scale_out=scale_out, bit=bit)
        for bit in range(nbits)
    ]
    input_grad, mixed_in, mixed_out = lax.switch(
        gossip_step[0] % nbits, branches, tokens[0], cotangent[0], w_in[0], w_out[0], rate
    )
    return (input_grad[None], mixed_in[None], mixed_out[None])


def solution(mesh):
    return jax.shard_map(
        per_device,
        mesh=mesh,
        in_specs=(
            P("rep", "tp", None),
            P("rep", "tp", None),
            P("rep", None, "tp"),
            P("rep", "tp", None),
            P(),
        ),
        out_specs=(P("rep", "tp", None), P("rep", None, "tp"), P("rep", "tp", None)),
        check_vma=False,
    )
```

```python
from functools import partial

import jax
import jax.numpy as jnp
from jax import lax
from jax.experimental import pallas as pl
from jax.experimental.pallas import tpu as pltpu
from jax.sharding import PartitionSpec as P


def from_partner(value, stride):
    mask = 2**stride
    pairs = [(source, source ^ mask) for source in range(lax.axis_size("rep"))]
    return lax.ppermute(value, "rep", pairs)


def after(value, *earlier):
    return lax.optimization_barrier((value, *earlier))[0]


def gelu_parts(preact):
    cdf = 0.5 * (1.0 + lax.erf(preact * 0.7071067811865476))
    dens = jnp.exp(-0.5 * preact * preact) * 0.3989422804014327
    return (preact * cdf, cdf + preact * dens)


def flip_size():
    return 2 if lax.axis_size("tp") % 2 == 0 else 1


def step_up(value):
    size, inner = lax.axis_size("tp"), flip_size()
    return lax.ppermute(value, "tp", [(i, (i + inner) % size) for i in range(size)])


def step_down(value):
    size, inner = lax.axis_size("tp"), flip_size()
    return lax.ppermute(value, "tp", [(i, (i - inner) % size) for i in range(size)])


def flip(value):
    return lax.ppermute(value, "tp", [(i, i ^ 1) for i in range(lax.axis_size("tp"))])


def short_ring():
    return lax.axis_size("tp") // flip_size() <= 4


def gather_slots(shard):
    inner = flip_size()
    ring = lax.axis_size("tp") // inner
    straight, flipped, current = [], [], shard
    for step in range(ring):
        if step:
            current = step_up(current)
        straight.append(current)
        if inner == 2:
            flipped.append(flip(current))
    return straight + flipped


def gather_rows(*shards):
    if not short_ring():
        return [lax.all_gather(shard, "tp", axis=0, tiled=True) for shard in shards]
    rows = shards[0].shape[0]
    slots = gather_slots(jnp.concatenate(shards, axis=0) if len(shards) > 1 else shards[0])
    return [
        jnp.concatenate([slot[n * rows : (n + 1) * rows] for slot in slots], axis=0)
        for n in range(len(shards))
    ]


def scatter_sum(halves, rows, pieces=()):
    pieces, given = list(pieces), ()

    def work(gate, *arrived):
        nonlocal given
        if not pieces:
            return arrived
        given = pieces.pop(0)(gate, given)
        arrived, given = lax.optimization_barrier((arrived, given))
        return arrived

    if not short_ring():
        whole = jnp.concatenate(halves, axis=0)
        done = lax.psum_scatter(whole, "tp", scatter_dimension=0, tiled=True)
        while pieces:
            work(halves[0])
        return done, given
    inner = flip_size()
    size = lax.axis_size("tp")
    ring = size // inner
    straight = halves[0] if inner == 2 else jnp.concatenate(halves, axis=0)
    slot = lambda number: straight[number * rows : (number + 1) * rows]
    sums = [slot(k).astype(jnp.float32) for k in range(ring)]
    if inner == 2:
        (arrived,) = work(halves[0], flip(halves[1]))
        sums = [
            own + arrived[k * rows : (k + 1) * rows].astype(jnp.float32) for k, own in enumerate(sums)
        ]
    leaving = [total.astype(jnp.bfloat16) for total in sums[1:]]
    arrived = [
        lax.ppermute(value, "tp", [(i, (i - k * inner) % size) for i in range(size)])
        for k, value in enumerate(leaving, 1)
    ]
    total = sums[0]
    if leaving:
        arrived = work(leaving[0], *arrived)
    for other in arrived:
        total = total + other.astype(jnp.float32)
    carried = total.astype(jnp.bfloat16)
    while pieces:
        work(carried)
    return carried, given


def dot_tn(left, right):
    return lax.dot_general(
        left, right, (((0,), (0,)), ((), ())), preferred_element_type=jnp.float32
    )


def dot_nt(left, right):
    return lax.dot_general(
        left, right, (((1,), (1,)), ((), ())), preferred_element_type=jnp.float32
    )


def mean_of(own, other):
    return ((own.astype(jnp.float32) + other.astype(jnp.float32)) * 0.5).astype(jnp.bfloat16)


def activations(tokens, upstream, w_in, w_out, scale_in, scale_out):
    preact = jnp.dot(tokens, w_in, preferred_element_type=jnp.float32) * scale_in
    value, slope = gelu_parts(preact)
    back = dot_nt(upstream, w_out) * scale_out
    return value.astype(jnp.bfloat16), (back * slope).astype(jnp.bfloat16)


def forward_kernel(*refs, slots, scale_in, scale_out):
    tok_slots, up_slots = refs[:slots], refs[slots : 2 * slots]
    w_in_ref, w_out_ref, both_ref, sides_out, tok_ref, up_ref, sems = refs[2 * slots :]
    step = pl.program_id(0)
    copies = [
        pltpu.make_async_copy(tok_ref, sides_out.at[0], sems.at[0]),
        pltpu.make_async_copy(up_ref, sides_out.at[1], sems.at[1]),
    ]

    @pl.when(step == 0)
    def _():
        for whole, parts, copy in zip((tok_ref, up_ref), (tok_slots, up_slots), copies):
            rows = parts[0].shape[0]
            for number, part in enumerate(parts):
                whole[number * rows : (number + 1) * rows, :] = part[...]
            copy.start()

    preact = jnp.dot(tok_ref[...], w_in_ref[...], preferred_element_type=jnp.float32) * scale_in
    back = dot_nt(up_ref[...], w_out_ref[...]) * scale_out
    value, slope = gelu_parts(preact)
    both_ref[0] = value.astype(jnp.bfloat16)
    both_ref[1] = (back * slope).astype(jnp.bfloat16)

    @pl.when(step == pl.num_programs(0) - 1)
    def _():
        for copy in copies:
            copy.wait()


def forward(tok_slots, up_slots, w_in, w_out, scale_in, scale_out):
    width, hid = w_in.shape
    slots, part_rows = len(tok_slots), tok_slots[0].shape[0]
    rows, cols = slots * part_rows, 256
    if rows > 256 or hid % cols:
        tokens, upstream = jnp.concatenate(tok_slots, axis=0), jnp.concatenate(up_slots, axis=0)
        both = activations(tokens, upstream, w_in, w_out, scale_in, scale_out)
        return jnp.stack(both), jnp.stack([tokens, upstream])
    once = pl.BlockSpec((part_rows, width), lambda i: (0, 0), pipeline_mode=pl.Buffered(1))
    return pl.pallas_call(
        partial(forward_kernel, slots=slots, scale_in=scale_in, scale_out=scale_out),
        grid=(hid // cols,),
        in_specs=[
            *[once] * (2 * slots),
            pl.BlockSpec((width, cols), lambda i: (0, i)),
            pl.BlockSpec((cols, width), lambda i: (i, 0)),
        ],
        out_specs=[
            pl.BlockSpec((2, rows, cols), lambda i: (0, 0, i)),
            pl.BlockSpec(memory_space=pl.ANY),
        ],
        out_shape=[
            jax.ShapeDtypeStruct((2, rows, hid), jnp.bfloat16),
            jax.ShapeDtypeStruct((2, rows, width), jnp.bfloat16),
        ],
        scratch_shapes=[
            pltpu.VMEM((rows, width), jnp.bfloat16),
            pltpu.VMEM((rows, width), jnp.bfloat16),
            pltpu.SemaphoreType.DMA((2,)),
        ],
        compiler_params=pltpu.CompilerParams(vmem_limit_bytes=48 << 20),
        cost_estimate=pl.CostEstimate(
            flops=4 * rows * width * hid, bytes_accessed=4 * width * hid, transcendentals=2 * rows * hid
        ),
        name="forward",
    )(*tok_slots, *up_slots, w_in, w_out)


def partial_kernel(dpre_ref, w_in_ref, first_ref, second_ref, *, scale_in):
    sums = (dot_nt(dpre_ref[...], w_in_ref[...]) * scale_in).astype(jnp.bfloat16)
    half = first_ref.shape[0]
    first_ref[...] = sums[:half]
    second_ref[...] = sums[half:]


def partial_sums(both, w_in, scale_in):
    _, rows, hid = both.shape
    width, half, size = w_in.shape[0], rows // 2, 1024
    if rows > 256 or width % size or half % 16:
        whole = (dot_nt(both[1], w_in) * scale_in).astype(jnp.bfloat16)
        return whole[:half], whole[half:]
    part = pl.BlockSpec((half, size), lambda i: (0, i))
    return pl.pallas_call(
        partial(partial_kernel, scale_in=scale_in),
        grid=(width // size,),
        in_specs=[
            pl.BlockSpec((None, rows, hid), lambda i: (1, 0, 0), pipeline_mode=pl.Buffered(1)),
            pl.BlockSpec((size, hid), lambda i: (i, 0)),
        ],
        out_specs=[part, part],
        out_shape=[jax.ShapeDtypeStruct((half, width), jnp.bfloat16)] * 2,
        compiler_params=pltpu.CompilerParams(vmem_limit_bytes=32 << 20),
        cost_estimate=pl.CostEstimate(
            flops=2 * rows * width * hid, bytes_accessed=2 * width * hid, transcendentals=0
        ),
        name="partial_sums",
    )(both, w_in)


def finish_kernel(
    factor_ref, own_ref, other_ref, left_ref, left2_ref, right_ref, right2_ref, out_ref, lefts_ref, rights_ref
):
    depth = left_ref.shape[0]

    @pl.when(pl.program_id(0) == 0)
    def _():
        rights_ref[:depth] = right_ref[...]
        rights_ref[depth:] = right2_ref[...]

    lefts_ref[:depth] = left_ref[...]
    lefts_ref[depth:] = left2_ref[...]
    grad = dot_tn(lefts_ref[...], rights_ref[...])
    both = own_ref[...].astype(jnp.float32) + other_ref[...].astype(jnp.float32)
    out_ref[...] = (0.5 * both - factor_ref[0] * grad).astype(jnp.bfloat16)


def block_rows(count, width):
    size = 128
    while size * 2 * width <= 1600 << 10 and size < 1024 and count % (size * 2) == 0:
        size *= 2
    return size


def finish(own, other, lefts, rights, factor):
    depth, width = rights[0][0].shape[1:]
    count = own.shape[0]
    size = block_rows(count, width)
    tile = pl.BlockSpec((size, width), lambda i: (i, 0))
    left = lambda place: pl.BlockSpec((None, depth, size), lambda i: (place, 0, i))
    right = lambda place: pl.BlockSpec(
        (None, depth, width), lambda i: (place, 0, 0), pipeline_mode=pl.Buffered(1)
    )
    return pl.pallas_call(
        finish_kernel,
        grid=(count // size,),
        in_specs=[
            pl.BlockSpec(memory_space=pltpu.SMEM),
            tile,
            tile,
            *[left(place) for _, place in lefts],
            *[right(place) for _, place in rights],
        ],
        out_specs=tile,
        out_shape=jax.ShapeDtypeStruct(own.shape, jnp.bfloat16),
        scratch_shapes=[
            pltpu.VMEM((2 * depth, size), jnp.bfloat16),
            pltpu.VMEM((2 * depth, width), jnp.bfloat16),
        ],
        compiler_params=pltpu.CompilerParams(vmem_limit_bytes=48 << 20),
        cost_estimate=pl.CostEstimate(
            flops=4 * depth * width * count, bytes_accessed=6 * width * count, transcendentals=0
        ),
        name="finish",
    )(factor.reshape(1), own, other, *[array for array, _ in lefts + rights])


def gather_both(tok, cot):
    if not short_ring():
        return [[lax.all_gather(shard, "tp", axis=0, tiled=True)] for shard in (tok, cot)]
    inner = flip_size()
    ring = lax.axis_size("tp") // inner
    current = [tok, cot]
    straight, flipped = [[], []], [[], []]
    for step in range(ring):
        for n in range(2):
            if step:
                held = current[n]
                if step > 1 and inner == 2:
                    held = after(held, flipped[n][step - 2])
                current[n] = step_up(held)
            straight[n].append(current[n])
        for n in range(2):
            if inner == 2 and n == 1 and ring > 2 and step == ring - 1:
                flipped[n].append(step_down(after(flipped[n][0], straight[n][-2])))
            elif inner == 2:
                held = after(current[n], flipped[n][-1]) if flipped[n] else current[n]
                flipped[n].append(flip(held))
    return straight[0] + flipped[0], straight[1] + flipped[1]


def near(tok, cot, w_in, w_out, rate, scale_in, scale_out, bit):
    rows = tok.shape[0]
    other_in = from_partner(w_in, bit)
    tok_slots, up_slots = gather_both(tok, cot)
    up_slots = [after(up_slots[0], other_in), *up_slots[1:]]
    both, sides = forward(tok_slots, up_slots, w_in, w_out, scale_in, scale_out)
    other_both = from_partner(both, bit)
    other_sides = from_partner(sides, bit)
    partials = partial_sums(both, w_in, scale_in)
    other_out = from_partner(after(w_out, other_both, other_sides, *partials), bit)
    stacks = [
        (w_in, other_in, ((sides, 0), (other_sides, 0)), ((both, 1), (other_both, 1)), 0.5 * rate * scale_in),
        (w_out, other_out, ((both, 0), (other_both, 0)), ((sides, 1), (other_sides, 1)), 0.5 * rate * scale_out),
    ]

    def piece(own, other, lefts, rights, factor):
        def run(gate, given):
            return (*given, finish(own, other, lefts, rights, after(factor, gate)))

        return run

    pieces = [piece(*stack) for stack in stacks]
    input_grad, (mixed_in, mixed_out) = scatter_sum(partials, rows, pieces)
    return input_grad, mixed_in, mixed_out


def update_kernel(factor_ref, own_ref, left_ref, right_ref, *out_refs, cuts):
    for out_ref, (lo, hi) in zip(out_refs, cuts):
        grad = dot_tn(left_ref[...], right_ref[:, lo:hi])
        out_ref[...] = (own_ref[:, lo:hi].astype(jnp.float32) - factor_ref[0] * grad).astype(jnp.bfloat16)


def update(own, left, right, factor, cuts):
    depth, width = right.shape
    count = own.shape[0]
    size = block_rows(count, width)
    return pl.pallas_call(
        partial(update_kernel, cuts=cuts),
        grid=(count // size,),
        in_specs=[
            pl.BlockSpec(memory_space=pltpu.SMEM),
            pl.BlockSpec((size, width), lambda i: (i, 0)),
            pl.BlockSpec((depth, size), lambda i: (0, i)),
            pl.BlockSpec((depth, width), lambda i: (0, 0), pipeline_mode=pl.Buffered(1)),
        ],
        out_specs=[pl.BlockSpec((size, hi - lo), lambda i: (i, 0)) for lo, hi in cuts],
        out_shape=[jax.ShapeDtypeStruct((count, hi - lo), jnp.bfloat16) for lo, hi in cuts],
        compiler_params=pltpu.CompilerParams(vmem_limit_bytes=48 << 20),
        cost_estimate=pl.CostEstimate(
            flops=2 * depth * width * count, bytes_accessed=4 * width * count, transcendentals=0
        ),
        name="update",
    )(factor.reshape(1), own, left, right)


def far(tok, cot, w_in, w_out, rate, scale_in, scale_out, bit):
    rows = tok.shape[0]
    unit = 128
    units = w_out.shape[0] // unit
    tok_other = from_partner(tok, bit)
    other_in = from_partner(w_in, bit)
    sent = [tok_other, other_in]

    def send(value):
        sent.append(from_partner(after(value, sent[-2]), bit))
        return sent[-1]

    tok_slots, up_slots = gather_both(tok, cot)
    both, sides = forward(tok_slots, up_slots, w_in, w_out, scale_in, scale_out)
    dpre = both[1]
    dpre_other = from_partner(after(dpre, tok_other), bit)
    (new_out,) = update(w_out, both[0], sides[1], rate * scale_out, ((0, w_out.shape[1]),))
    partials = partial_sums(after(both, new_out), w_in, scale_in)
    input_grad, _ = scatter_sum(partials, rows)
    tokens_other = gather_rows(after(tok_other, input_grad))[0]
    marks = [0, units // 4, units // 2, 3 * units // 4, units - 1, units]
    marks = [mark * unit for mark in marks]
    marks[-2] += unit // 2
    cuts = [(lo, hi) for lo, hi in zip(marks, marks[1:]) if lo < hi]
    mixed_in, mixed_out = None, jnp.zeros_like(w_out)
    for number, (lo, hi) in enumerate(cuts):
        own = new_out[lo:hi]
        other = send(own)
        mixed_out = lax.dynamic_update_slice(mixed_out, mean_of(own, other), (lo, 0))
        if number == 0:
            factor = after(0.5 * rate * scale_in, other)
            lefts = ((sides, 0), (tokens_other[None], 0))
            rights = ((both, 1), (dpre_other[None], 0))
            mixed_in = finish(w_in, other_in, lefts, rights, factor)
    return input_grad, mixed_in, mixed_out


def per_device(tokens, cotangent, w_in, w_out, gossip_step):
    width = tokens.shape[2]
    hid_dev = w_in.shape[2]
    scale_in = 1.0 / width**0.5
    scale_out = 1.0 / (hid_dev * lax.axis_size("tp")) ** 0.5
    rate = 16.0 / (8.0 + gossip_step[0].astype(jnp.float32))
    nbits = lax.axis_size("rep").bit_length() - 1
    branches = [
        partial(near if bit == 0 else far, scale_in=scale_in, scale_out=scale_out, bit=bit)
        for bit in range(nbits)
    ]
    input_grad, mixed_in, mixed_out = lax.switch(
        gossip_step[0] % nbits, branches, tokens[0], cotangent[0], w_in[0], w_out[0], rate
    )
    return (input_grad[None], mixed_in[None], mixed_out[None])


def solution(mesh):
    return jax.shard_map(
        per_device,
        mesh=mesh,
        in_specs=(
            P("rep", "tp", None),
            P("rep", "tp", None),
            P("rep", None, "tp"),
            P("rep", "tp", None),
            P(),
        ),
        out_specs=(P("rep", "tp", None), P("rep", None, "tp"), P("rep", "tp", None)),
        check_vma=False,
    )
```
